1024 devices in a mesh: ctx: 128 (over y, z), tp: 8 (over x, core).
Axes of the slice: x: 4, y: 4, z: 32, core: 2. Of those that a mesh axis runs over, the one named last changes fastest.
Arguments:
- tokens: bfloat16 [32768, 2048], P('ctx'), may hold values from -6 to 6
- w_query: bfloat16 [2048, 4096], P(None, 'tp'), may hold values from -0.125 to 0.125
- w_key: bfloat16 [2048, 512], replicated, may hold values from -0.125 to 0.125
- w_value: bfloat16 [2048, 512], replicated, may hold values from -0.125 to 0.125
- w_out: bfloat16 [4096, 2048], P('tp'), may hold values from -0.09375 to 0.09375
- query_gain: float32 [128], replicated, may hold values from 0.5 to 2
- key_gain: float32 [128], replicated, may hold values from 0.5 to 2
- doc_lengths: int32 [256], replicated, may hold values from 1 to 4096, as said below
Outputs:
- layer_out: bfloat16 [32768, 2048], P('ctx', 'tp')
The draws below stay inside these ranges and needn't reach their ends.
Inputs may be any that keep to these rules, and one draw needn't show every extreme that they name: `doc_lengths`: the lengths sum to 32768; the second-to-last document has exactly 4096 tokens and the last one exactly 128.
All inputs are finite; a program needn't handle non-finite values.
Results may differ from the reference program's by a relative error of at most 0.014.
Values may be sent and summed in bfloat16 or wider, within the bound.
No kernel may reach another device: no remote copies, remote signals or barrier semaphores. Data moves between devices by JAX's collectives and lax.ppermute only.
A program may use at most 32 MiB of HBM per device.

```python
import math
import jax
import jax.numpy as jnp
from jax import lax

D = 2048
H = 32
KVH = 4
HD = 128
TOK_DEV = 256
TOKENS = 32768
REACH = 16
MAXDOC = 4096
DOCS = 256
N_TP = 8


def draw_doc_lengths(key, part):
    rest_count = DOCS - 2
    tail_doc = TOK_DEV // 2
    spare = TOKENS - MAXDOC - tail_doc - rest_count
    long_count = max(2, DOCS // 32)
    long_budget = spare * 3 // 4
    order = jax.random.permutation(jax.random.fold_in(key, 23), rest_count).astype(jnp.int32)
    chosen = order[:long_count]
    is_long = jnp.zeros((rest_count,), jnp.int32).at[chosen].set(1)
    long_pick = MAXDOC // 4 + jax.random.randint(jax.random.fold_in(key, 29), (rest_count,), 0, MAXDOC - MAXDOC // 4).astype(jnp.int32)
    long_draw = (long_pick * is_long).astype(jnp.int32)
    long_total = jnp.sum(long_draw).astype(jnp.int32)
    scaled = jnp.where(long_total > long_budget, long_draw * long_budget // jnp.maximum(long_total, 1), long_draw).astype(jnp.int32)
    remaining = (spare - jnp.sum(scaled)).astype(jnp.int32)
    short_mask = (1 - is_long).astype(jnp.int32)
    weights = (jax.random.randint(jax.random.fold_in(key, 17), (rest_count,), 1, 9).astype(jnp.int32) * short_mask).astype(jnp.int32)
    short_extra = (remaining * weights // jnp.sum(weights)).astype(jnp.int32)
    leftover = (remaining - jnp.sum(short_extra)).astype(jnp.int32)
    short_rank = (jnp.cumsum(short_mask) - 1).astype(jnp.int32)
    bump = (short_mask * (short_rank < leftover).astype(jnp.int32)).astype(jnp.int32)
    extra = (scaled + short_extra + bump).astype(jnp.int32)
    long_doc = jnp.full((1,), MAXDOC, jnp.int32)
    last_doc = jnp.full((1,), tail_doc, jnp.int32)
    return jnp.concatenate([(1 + extra).astype(jnp.int32), long_doc, last_doc])


def steps_of(own_key, extent, pieces, smallest, top_value):
    def one(position, parts):
        steps = jax.random.uniform(jax.random.fold_in(jax.random.fold_in(own_key, 6), position), (parts,), jnp.float32, smallest / len(pieces), top_value / len(pieces))
        return jnp.repeat(jnp.exp(steps), extent[position] // parts).reshape((-1,) + (1,) * (len(extent) - position - 1))

    loudness = one(*pieces[0])
    for cut in pieces[1:]:
        loudness = loudness * one(*cut)
    return loudness


def noise(rng, shape, scale, bound, pieces=(), kind=jnp.bfloat16):
    values = jax.random.normal(rng, shape, jnp.float32) * scale
    if len(pieces) > 0:
        values = steps_of(rng, shape, pieces, -0.22, 0.18) * values
    return jnp.clip(values, min=-bound, max=bound).astype(kind)


def setup_inputs(seed: int = 0) -> dict:
    key_of = jax.random.split(jax.random.key(seed), 9)
    tokens = noise(key_of[0], (TOKENS, D), 1.0, 6.0, ((0, 128),))
    w_query = noise(key_of[1], (D, H * HD), D ** -0.5, 0.125, ((1, 8),))
    w_key = noise(key_of[2], (D, KVH * HD), D ** -0.5, 0.125)
    w_value = noise(key_of[3], (D, KVH * HD), D ** -0.5, 0.125)
    w_out = noise(key_of[4], (H * HD, D), (H * HD) ** -0.5, 0.09375, ((0, 8),))
    query_gain = jnp.clip(jnp.exp(jax.random.uniform(key_of[5], (HD,), jnp.float32, math.log(0.5), math.log(2.0))), 0.5, 2.0)
    key_gain = jnp.clip(jnp.exp(jax.random.uniform(key_of[6], (HD,), jnp.float32, math.log(0.5), math.log(2.0))), 0.5, 2.0)
    doc_lengths = draw_doc_lengths(jax.random.fold_in(key_of[8], 71), 0)
    return {"tokens": tokens, "w_query": w_query, "w_key": w_key, "w_value": w_value, "w_out": w_out, "query_gain": query_gain, "key_gain": key_gain, "doc_lengths": doc_lengths}


EPSILON = 1e-06
ROPE_BASE = 1000000.0
NEGATIVE = -1e+30

def doc_starts(positions, doc_lengths):
    doc_ends = jnp.cumsum(doc_lengths).astype(jnp.int32)
    before = doc_ends[None, :] <= positions[:, None]
    return lax.optimization_barrier(jnp.sum(jnp.where(before, doc_lengths[None, :], 0), axis=1)).astype(jnp.int32)

def norm_rotate(inputs, gain_vec, offsets):
    full_width = inputs.shape[-1]
    half_width = full_width // 2
    inv_norm = lax.rsqrt(lax.optimization_barrier(jnp.mean(inputs * inputs, axis=-1, keepdims=True)) + EPSILON)
    normed = inputs * inv_norm * gain_vec
    frequency = ROPE_BASE ** (-2.0 * jnp.arange(half_width, dtype=jnp.float32) / full_width)
    angles = offsets[:, None] * frequency[None, :]
    cosine = jnp.cos(angles)[:, None, :]
    sine_part = jnp.sin(angles)[:, None, :]
    first_half = normed[..., :half_width]
    second_half = normed[..., half_width:]
    return jnp.concatenate([first_half * cosine - second_half * sine_part, second_half * cosine + first_half * sine_part], axis=-1)

def reference(tokens, w_query, w_key, w_value, w_out, query_gain, key_gain, doc_lengths):
    positions = jnp.arange(TOKENS, dtype=jnp.int32)
    starts_all = doc_starts(positions, doc_lengths)
    offsets = (positions - starts_all).astype(jnp.float32)
    queries = norm_rotate(jnp.dot(tokens, w_query, preferred_element_type=jnp.float32).reshape(TOKENS, H, HD), query_gain, offsets).astype(jnp.bfloat16)
    keys_all = norm_rotate(jnp.dot(tokens, w_key, preferred_element_type=jnp.float32).reshape(TOKENS, KVH, HD), key_gain, offsets).astype(jnp.bfloat16)
    values_all = jnp.dot(tokens, w_value, preferred_element_type=jnp.float32).astype(jnp.bfloat16).reshape(TOKENS, KVH, HD)
    key_span = REACH * TOK_DEV
    padding = jnp.zeros((key_span, KVH, HD), jnp.bfloat16)
    keys_padded = jnp.concatenate([padding, keys_all], axis=0)
    values_padded = jnp.concatenate([padding, values_all], axis=0)
    group_size = H // KVH

    def attend_block(block_index):
        start_row = (block_index * TOK_DEV).astype(jnp.int32)
        query_block = lax.dynamic_slice_in_dim(queries, start_row, TOK_DEV, 0).astype(jnp.float32).reshape(TOK_DEV, KVH, group_size, HD)
        key_block = lax.dynamic_slice_in_dim(keys_padded, start_row, key_span + TOK_DEV, 0).astype(jnp.float32)
        value_block = lax.dynamic_slice_in_dim(values_padded, start_row, key_span + TOK_DEV, 0).astype(jnp.float32)
        query_pos = start_row + jnp.arange(TOK_DEV, dtype=jnp.int32)
        query_start = lax.dynamic_slice_in_dim(starts_all, start_row, TOK_DEV, 0)
        key_pos = start_row - key_span + jnp.arange(key_span + TOK_DEV, dtype=jnp.int32)
        visible = (key_pos[None, :] <= query_pos[:, None]) & (key_pos[None, :] >= query_start[:, None])
        scores = jnp.einsum('tgjd,sgd->gjts', query_block, key_block) * HD ** (-0.5)
        row_peak = lax.optimization_barrier(jnp.max(jnp.where(visible, scores, NEGATIVE), axis=-1, keepdims=True))
        weights = jnp.where(visible, jnp.exp(scores - row_peak), 0.0)
        row_total = lax.optimization_barrier(jnp.sum(weights, axis=-1))
        rounded = lax.optimization_barrier(weights.astype(jnp.bfloat16)).astype(jnp.float32)
        mixed = jnp.einsum('gjts,sgd->tgjd', rounded, value_block)
        mixed = mixed / jnp.transpose(row_total, (2, 0, 1))[..., None]
        return mixed.reshape(TOK_DEV, H * HD).astype(jnp.bfloat16)
    attended = lax.map(attend_block, jnp.arange(TOKENS // TOK_DEV, dtype=jnp.int32)).reshape(TOKENS, H * HD)
    group_cols = H // N_TP * HD
    summed = jnp.zeros((TOKENS, D), jnp.float32)
    for tp_rank in range(N_TP):
        head_term = jnp.dot(attended[:, tp_rank * group_cols:(tp_rank + 1) * group_cols], w_out[tp_rank * group_cols:(tp_rank + 1) * group_cols], preferred_element_type=jnp.float32)
        summed = summed + lax.optimization_barrier(head_term.astype(jnp.bfloat16)).astype(jnp.float32)
    return summed.astype(jnp.bfloat16)
```

```python
import functools

import jax
import jax.numpy as jnp
from jax import lax
from jax.experimental import pallas as pl
from jax.experimental.pallas import tpu as pltpu
from jax.sharding import Mesh, PartitionSpec as P

H = 32
KVH = 4
HD = 128
REACH = 16
LINE = 4
EPSILON = 1e-06
ROPE_BASE = 1000000.0
LOG2E = 1.4426950408889634

CTX = ("y", "zh", "zl")
TP = ("x", "c")
VMEM = pltpu.VMEM


def doc_starts(positions, doc_lengths):
    doc_ends = jnp.cumsum(doc_lengths)
    before = doc_ends[None, :] <= positions[:, None]
    return jnp.sum(jnp.where(before, doc_lengths[None, :], 0), axis=1)


def norm_rotate(u, gain, cosine, sine):
    inv = lax.rsqrt(jnp.mean(u * u, axis=-1, keepdims=True) + EPSILON)
    w = u * inv * gain
    return w * cosine + pltpu.roll(w, HD // 2, 1) * sine


def kv_body(info, tokens, w_key, w_value, gain, cosine, sine, out):
    @pl.when(info[1] == 0)
    def _():
        u = jnp.dot(tokens[...], w_key[...], preferred_element_type=jnp.float32)
        out[...] = norm_rotate(u, gain[...], cosine[...], sine[...]).astype(out.dtype)

    @pl.when(info[1] != 0)
    def _():
        u = jnp.dot(tokens[...], w_value[...], preferred_element_type=jnp.float32)
        out[...] = u.astype(out.dtype)


def project_kv(info, tokens, w_key, w_value, gain, cosine, sine):
    rows, width = tokens.shape
    head = pl.BlockSpec((width, HD), lambda i, s: (0, s[0]))

    def whole(a):
        return pl.BlockSpec(a.shape, lambda i, s: (0,) * a.ndim)

    return pl.pallas_call(
        kv_body,
        out_shape=jax.ShapeDtypeStruct((rows, HD), jnp.bfloat16),
        grid_spec=pltpu.PrefetchScalarGridSpec(
            num_scalar_prefetch=1,
            grid=(1,),
            in_specs=[whole(tokens), head, head, whole(gain), whole(cosine), whole(sine)],
            out_specs=pl.BlockSpec((rows, HD), lambda i, s: (0, 0)),
        ),
        cost_estimate=pl.CostEstimate(
            flops=2 * rows * width * HD, bytes_accessed=2 * rows * width, transcendentals=0
        ),
        name="project_kv",
    )(info, tokens, w_key, w_value, gain, cosine, sine)


def q_body(heads, tokens, w_query, gain, cosine, sine, out):
    u = jnp.dot(tokens[...], w_query[...], preferred_element_type=jnp.float32)
    for h in range(heads):
        part = u[:, h * HD : (h + 1) * HD]
        out[h] = norm_rotate(part, gain[...], cosine[...], sine[...]).astype(out.dtype)


def project_q(tokens, w_query, gain, cosine, sine):
    rows, width = tokens.shape
    heads = w_query.shape[1] // HD
    return pl.pallas_call(
        functools.partial(q_body, heads),
        out_shape=jax.ShapeDtypeStruct((heads, rows, HD), jnp.bfloat16),
        in_specs=[pl.BlockSpec(memory_space=VMEM)] * 5,
        out_specs=pl.BlockSpec(memory_space=VMEM),
        cost_estimate=pl.CostEstimate(
            flops=2 * rows * width * heads * HD, bytes_accessed=6 * rows * width, transcendentals=0
        ),
        name="project_q",
    )(tokens, w_query, gain, cosine, sine)


def add_block(heads, queries, key, value, total, weighted, mask):
    for h in range(heads):
        scores = lax.dot_general(
            queries[h], key, (((1,), (1,)), ((), ())), preferred_element_type=jnp.float32
        )
        weights = jnp.exp2(scores * (HD**-0.5 * LOG2E))
        if mask is not None:
            weights = weights * mask[...]
        total[h] += weights[:, :HD] + weights[:, HD:]
        weighted[h] += jnp.dot(
            weights.astype(jnp.bfloat16), value, preferred_element_type=jnp.float32
        )


def attend_body(heads, info, queries, kv, starts, w_out, out, total, weighted, mask, attended):
    rows = queries.shape[1]
    block, first, last = info[0], info[1], info[2]
    total[...] = jnp.zeros_like(total)
    weighted[...] = jnp.zeros_like(weighted)
    group = block // LINE

    def step(b, carry):
        back = group - b // LINE
        place = (b % LINE) * 2
        key, value = kv[place, back], kv[place + 1, back]
        whole = (b < block) & (b * rows >= last)

        @pl.when(whole)
        def _():
            add_block(heads, queries, key, value, total, weighted, None)

        @pl.when(jnp.logical_not(whole))
        def _():
            key_pos = b * rows + lax.broadcasted_iota(jnp.int32, (rows, rows), 1)
            query_pos = block * rows + lax.broadcasted_iota(jnp.int32, (rows, rows), 0)
            visible = (key_pos <= query_pos) & (key_pos >= starts[...])
            mask[...] = jnp.where(visible, 1.0, 0.0)
            add_block(heads, queries, key, value, total, weighted, mask)

        return carry

    lax.fori_loop(first // rows, block + 1, step, 0)
    for h in range(heads):
        sums = jnp.sum(total[h], axis=1, keepdims=True)
        attended[:, h * HD : (h + 1) * HD] = (weighted[h] / sums).astype(attended.dtype)
    out[...] = jnp.dot(
        attended[...], w_out[...], preferred_element_type=jnp.float32
    ).astype(out.dtype)


def attend(info, queries, kv, starts, w_out):
    heads, rows, _ = queries.shape
    return pl.pallas_call(
        functools.partial(attend_body, heads),
        out_shape=jax.ShapeDtypeStruct((rows, w_out.shape[1]), jnp.bfloat16),
        in_specs=[pl.BlockSpec(memory_space=pltpu.SMEM)] + [pl.BlockSpec(memory_space=VMEM)] * 4,
        out_specs=pl.BlockSpec(memory_space=VMEM),
        scratch_shapes=[
            VMEM((heads, rows, HD), jnp.float32),
            VMEM((heads, rows, HD), jnp.float32),
            VMEM((rows, rows), jnp.float32),
            VMEM((rows, heads * HD), jnp.bfloat16),
        ],
        cost_estimate=pl.CostEstimate(
            flops=(REACH + 1) * 4 * heads * rows * rows * HD, bytes_accessed=4 << 20, transcendentals=0
        ),
        name="attend",
    )(info, queries, kv, starts, w_out)


def local(tokens, w_query, w_key, w_value, w_out, query_gain, key_gain, doc_lengths):
    rows = tokens.shape[0]
    heads = w_query.shape[1] // HD
    tp_rank = lax.axis_index(TP)
    block = lax.axis_index(CTX)
    core = lax.axis_index("c")
    kv_head = tp_rank * heads // (H // KVH)
    positions = block * rows + jnp.arange(rows, dtype=jnp.int32)
    starts = doc_starts(positions, doc_lengths)
    offsets = (positions - starts).astype(jnp.float32)
    half = HD // 2
    frequency = ROPE_BASE ** (-2.0 * jnp.arange(half, dtype=jnp.float32) / HD)
    angles = offsets[:, None] * frequency[None, :]
    cosine = jnp.cos(angles)
    sine = jnp.sin(angles)
    cosine = jnp.concatenate([cosine, cosine], axis=1)
    sine = jnp.concatenate([-sine, sine], axis=1)
    info = jnp.stack([kv_head, core]).astype(jnp.int32)
    part = project_kv(info, tokens, w_key, w_value, key_gain[None], cosine, sine)
    queries = project_q(tokens, w_query, query_gain[None], cosine, sine)

    groups = lax.axis_size("y") * lax.axis_size("zh")
    onward = [(i, (i + 1) % groups) for i in range(groups)]
    parts = [part]
    for _ in range(REACH // LINE):
        parts.append(lax.ppermute(parts[-1], ("y", "zh"), onward))
    kv = lax.all_gather(jnp.stack(parts), ("zl", "c"), axis=0)

    info = jnp.stack([block, starts[0], starts[rows - 1]]).astype(jnp.int32)
    head_term = attend(info, queries, kv, starts[:, None], w_out)
    return lax.psum_scatter(head_term, TP, scatter_dimension=1, tiled=True)


def solution(mesh):
    ctx, tp = mesh.shape["ctx"], mesh.shape["tp"]
    y = max(1, ctx // 32)
    devices = mesh.devices.reshape(y, ctx // (y * LINE), LINE, tp // 2, 2)
    fine = Mesh(devices, CTX + TP)
    return jax.shard_map(
        local,
        mesh=fine,
        in_specs=(P(CTX, None), P(None, TP), P(), P(), P(TP, None), P(), P(), P()),
        out_specs=P(CTX, TP),
        check_vma=False,
    )
```

```python
import functools

import jax
import jax.numpy as jnp
from jax import lax
from jax.experimental import pallas as pl
from jax.experimental.pallas import tpu as pltpu
from jax.sharding import Mesh, PartitionSpec as P

H = 32
KVH = 4
HD = 128
REACH = 16
LINE = 4
EPSILON = 1e-06
ROPE_BASE = 1000000.0
LOG2E = 1.4426950408889634

TP = ("x", "c")
VMEM = pltpu.VMEM


def doc_starts(positions, doc_lengths):
    doc_ends = jnp.cumsum(doc_lengths)
    before = doc_ends[None, :] <= positions[:, None]
    return jnp.sum(jnp.where(before, doc_lengths[None, :], 0), axis=1)


def norm_rotate(u, gain, cosine, sine):
    inv = lax.rsqrt(jnp.mean(u * u, axis=-1, keepdims=True) + EPSILON)
    w = u * inv * gain
    return w * cosine + pltpu.roll(w, HD // 2, 1) * sine


def kv_body(info, tokens, w_key, w_value, gain, cosine, sine, out):
    @pl.when(info[1] == 0)
    def _():
        u = jnp.dot(tokens[...], w_key[...], preferred_element_type=jnp.float32)
        out[...] = norm_rotate(u, gain[...], cosine[...], sine[...]).astype(out.dtype)

    @pl.when(info[1] != 0)
    def _():
        u = jnp.dot(tokens[...], w_value[...], preferred_element_type=jnp.float32)
        out[...] = u.astype(out.dtype)


def project_kv(info, tokens, w_key, w_value, gain, cosine, sine):
    rows, width = tokens.shape
    head = pl.BlockSpec((width, HD), lambda i, s: (0, s[0]))

    def whole(a):
        return pl.BlockSpec(a.shape, lambda i, s: (0,) * a.ndim)

    return pl.pallas_call(
        kv_body,
        out_shape=jax.ShapeDtypeStruct((rows, HD), jnp.bfloat16),
        grid_spec=pltpu.PrefetchScalarGridSpec(
            num_scalar_prefetch=1,
            grid=(1,),
            in_specs=[whole(tokens), head, head, whole(gain), whole(cosine), whole(sine)],
            out_specs=pl.BlockSpec((rows, HD), lambda i, s: (0, 0)),
        ),
        cost_estimate=pl.CostEstimate(
            flops=2 * rows * width * HD, bytes_accessed=2 * rows * width, transcendentals=0
        ),
        compiler_params=pltpu.CompilerParams(vmem_limit_bytes=10 << 20),
        name="project_kv",
    )(info, tokens, w_key, w_value, gain, cosine, sine)


def q_body(heads, tokens, w_query, gain, cosine, sine, out):
    u = jnp.dot(tokens[...], w_query[...], preferred_element_type=jnp.float32)
    for h in range(heads):
        part = u[:, h * HD : (h + 1) * HD]
        out[h] = norm_rotate(part, gain[...], cosine[...], sine[...]).astype(out.dtype)


def project_q(tokens, w_query, gain, cosine, sine):
    rows, width = tokens.shape
    heads = w_query.shape[1] // HD
    return pl.pallas_call(
        functools.partial(q_body, heads),
        out_shape=jax.ShapeDtypeStruct((heads, rows, HD), jnp.bfloat16),
        in_specs=[pl.BlockSpec(memory_space=VMEM)] * 5,
        out_specs=pl.BlockSpec(memory_space=VMEM),
        cost_estimate=pl.CostEstimate(
            flops=2 * rows * width * heads * HD, bytes_accessed=6 * rows * width, transcendentals=0
        ),
        compiler_params=pltpu.CompilerParams(vmem_limit_bytes=10 << 20),
        name="project_q",
    )(tokens, w_query, gain, cosine, sine)


def add_block(heads, queries, key, value, total, weighted, mask):
    for h in range(heads):
        scores = lax.dot_general(
            queries[h], key, (((1,), (1,)), ((), ())), preferred_element_type=jnp.float32
        )
        weights = jnp.exp2(scores * (HD**-0.5 * LOG2E))
        if mask is not None:
            weights = weights * mask[...]
        total[h] += weights[:, :HD] + weights[:, HD:]
        weighted[h] += jnp.dot(
            weights.astype(jnp.bfloat16), value, preferred_element_type=jnp.float32
        )


def attend_body(heads, counts, info, queries, starts, *refs):
    n = len(counts)
    mine, theirs, refs = refs[:n], refs[n : 2 * n], refs[2 * n :]
    w_out_any, keep, give, total, weighted, mask, attended, kv, w_out, sems = refs
    rows = queries.shape[1]
    block, first, last, core = info[0], info[1], info[2], info[3]
    copies = []
    for side, group in ((core, mine), (1 - core, theirs)):
        at = 0
        for ref, count in zip(group, counts):
            copies.append(
                pltpu.make_async_copy(
                    ref, kv.at[side, pl.ds(at, count)], sems.at[len(copies)]
                )
            )
            at += count
    weights_copy = pltpu.make_async_copy(w_out_any, w_out, sems.at[len(copies)])
    for copy in copies:
        copy.start()
    weights_copy.start()
    total[...] = jnp.zeros_like(total)
    weighted[...] = jnp.zeros_like(weighted)
    for copy in copies:
        copy.wait()

    def step(b, carry):
        back = block - b
        place = jnp.where(back == REACH, REACH, (back % LINE) * LINE + back // LINE)
        key, value = kv[0, place], kv[1, place]
        whole = (b < block) & (b * rows >= last)

        @pl.when(whole)
        def _():
            add_block(heads, queries, key, value, total, weighted, None)

        @pl.when(jnp.logical_not(whole))
        def _():
            key_pos = b * rows + lax.broadcasted_iota(jnp.int32, (rows, rows), 1)
            query_pos = block * rows + lax.broadcasted_iota(jnp.int32, (rows, rows), 0)
            visible = (key_pos <= query_pos) & (key_pos >= starts[...])
            mask[...] = jnp.where(visible, 1.0, 0.0)
            add_block(heads, queries, key, value, total, weighted, mask)

        return carry

    lax.fori_loop(first // rows, block + 1, step, 0)
    for h in range(heads):
        sums = jnp.sum(total[h], axis=1, keepdims=True)
        attended[:, h * HD : (h + 1) * HD] = (weighted[h] / sums).astype(attended.dtype)
    weights_copy.wait()
    width = keep.shape[2]
    for out, side in ((give, 1 - core), (keep, core)):
        for x in range(keep.shape[0]):
            columns = pl.ds(pl.multiple_of((2 * x + side) * width, width), width)
            out[x] = jnp.dot(
                attended[...], w_out[:, columns], preferred_element_type=jnp.float32
            ).astype(out.dtype)


def attend(info, queries, starts, mine, theirs, w_out, chips):
    heads, rows, _ = queries.shape
    counts = [a.shape[0] for a in mine]
    width = w_out.shape[1] // (2 * chips)
    half = jax.ShapeDtypeStruct((chips, rows, width), jnp.bfloat16)
    return pl.pallas_call(
        functools.partial(attend_body, heads, counts),
        out_shape=(half, half),
        in_specs=[pl.BlockSpec(memory_space=pltpu.SMEM)]
        + [pl.BlockSpec(memory_space=VMEM)] * 2
        + [pl.BlockSpec(memory_space=pl.ANY)] * (2 * len(counts) + 1),
        out_specs=(pl.BlockSpec(memory_space=VMEM),) * 2,
        scratch_shapes=[
            VMEM((heads, rows, HD), jnp.float32),
            VMEM((heads, rows, HD), jnp.float32),
            VMEM((rows, rows), jnp.float32),
            VMEM((rows, heads * HD), jnp.bfloat16),
            VMEM((2, REACH + 1, rows, HD), jnp.bfloat16),
            VMEM(w_out.shape, jnp.bfloat16),
            pltpu.SemaphoreType.DMA((2 * len(counts) + 1,)),
        ],
        cost_estimate=pl.CostEstimate(
            flops=(REACH + 1) * 4 * heads * rows * rows * HD, bytes_accessed=4 << 20, transcendentals=0
        ),
        compiler_params=pltpu.CompilerParams(vmem_limit_bytes=16 << 20),
        name="attend",
    )(info, queries, starts, *mine, *theirs, w_out)


def passed_along(a, distance):
    n = lax.axis_size("ctx")
    return lax.ppermute(a, "ctx", [(i, (i + distance) % n) for i in range(n)])


def swapped(a):
    return lax.ppermute(a, "c", [(0, 1), (1, 0)])


def local(tokens, w_query, w_key, w_value, w_out, query_gain, key_gain, doc_lengths):
    rows = tokens.shape[0]
    heads = w_query.shape[1] // HD
    tp_rank = lax.axis_index(TP)
    block = lax.axis_index("ctx")
    core = lax.axis_index("c")
    kv_head = tp_rank * heads // (H // KVH)
    positions = block * rows + jnp.arange(rows, dtype=jnp.int32)
    starts = doc_starts(positions, doc_lengths)
    offsets = (positions - starts).astype(jnp.float32)
    half = HD // 2
    frequency = ROPE_BASE ** (-2.0 * jnp.arange(half, dtype=jnp.float32) / HD)
    angles = offsets[:, None] * frequency[None, :]
    cosine = jnp.cos(angles)
    sine = jnp.sin(angles)
    cosine = jnp.concatenate([cosine, cosine], axis=1)
    sine = jnp.concatenate([-sine, sine], axis=1)
    info = jnp.stack([kv_head, core]).astype(jnp.int32)
    part = project_kv(info, tokens, w_key, w_value, key_gain[None], cosine, sine)
    queries = project_q(tokens, w_query, query_gain[None], cosine, sine)

    far = [part]
    for _ in range(REACH // LINE):
        far.append(passed_along(far[-1], LINE))
    rest = far.pop()[None]
    mine = [jnp.stack(far)]
    for _ in range(LINE - 1):
        mine.append(passed_along(mine[-1], 1))
    mine[-1] = jnp.concatenate([mine[-1], rest])
    theirs = [swapped(a) for a in mine]

    info = jnp.stack([block, starts[0], starts[rows - 1], core]).astype(jnp.int32)
    keep, give = attend(info, queries, starts[:, None], mine, theirs, w_out, lax.axis_size("x"))
    pairs = (keep.astype(jnp.float32) + swapped(give).astype(jnp.float32)).astype(jnp.bfloat16)
    terms = lax.all_to_all(pairs, "x", 0, 0, tiled=True)
    return jnp.sum(terms.astype(jnp.float32), axis=0).astype(jnp.bfloat16)


def solution(mesh):
    ctx, tp = mesh.shape["ctx"], mesh.shape["tp"]
    fine = Mesh(mesh.devices.reshape(ctx, tp // 2, 2), ("ctx",) + TP)
    return jax.shard_map(
        local,
        mesh=fine,
        in_specs=(P("ctx", None), P(None, TP), P(), P(), P(TP, None), P(), P(), P()),
        out_specs=P("ctx", TP),
        check_vma=False,
    )
```

```python
import functools

import jax
import jax.numpy as jnp
import numpy as np
from jax import lax
from jax.experimental import pallas as pl
from jax.experimental.pallas import tpu as pltpu
from jax.sharding import Mesh, PartitionSpec as P


H = 32
KVH = 4
HD = 128
LINE = 4
EPSILON = 1e-06
ROPE_BASE = 1000000.0
LOG2E = 1.4426950408889634

TP = ("x", "c")
VMEM = pltpu.VMEM
FREQUENCY = ROPE_BASE ** (-2.0 * np.arange(HD // 2, dtype=np.float64) / HD)


def norm_rotate(u, gain, cosine, sine):
    inv = lax.rsqrt(jnp.mean(u * u, axis=-1, keepdims=True) + EPSILON)
    w = u * inv * gain
    return w * cosine + pltpu.roll(w, HD // 2, 1) * sine


def iota(shape, axis):
    return lax.broadcasted_iota(jnp.int32, shape, axis)


def kv_body(
    heads, tokens_hbm, w_key, w_value, gain, lengths, frequency,
    out, cosine, sine, starts, span, tokens, weight, sems,
):
    rows = out.shape[0]
    docs = lengths.shape[1]
    core = lax.axis_index("c")
    block = lax.axis_index("ctx")
    head = (2 * lax.axis_index("x") + core) * heads // (H // KVH)
    columns = pl.ds(pl.multiple_of(head * HD, HD), HD)
    tokens_copy = pltpu.make_async_copy(tokens_hbm, tokens, sems.at[0])
    tokens_copy.start()

    @pl.when(core == 0)
    def _():
        pltpu.make_async_copy(w_key.at[:, columns], weight, sems.at[1]).start()

    @pl.when(core != 0)
    def _():
        pltpu.make_async_copy(w_value.at[:, columns], weight, sems.at[1]).start()

    counts = lengths[...].astype(jnp.float32)
    before = iota((docs, docs), 1) <= iota((docs, docs), 0)
    ends = jnp.sum(jnp.where(before, counts, 0.0), axis=1, keepdims=True)
    here = (block * rows + iota((docs, rows), 1)).astype(jnp.float32)
    start_row = jnp.max(jnp.where(ends <= here, ends, 0.0), axis=0, keepdims=True)
    same = iota((rows, rows), 0) == iota((rows, rows), 1)
    start_column = jnp.sum(jnp.where(same, start_row, 0.0), axis=1, keepdims=True)
    starts[...] = start_column.astype(jnp.int32)
    span[0] = jnp.min(start_row).astype(jnp.int32)
    span[1] = jnp.max(start_row).astype(jnp.int32)
    offsets = (block * rows + iota((rows, 1), 0)).astype(jnp.float32) - start_column
    angles = offsets * frequency[...]
    cosine[...] = jnp.cos(angles)
    lower = iota((rows, HD), 1) < HD // 2
    turned = jnp.sin(angles)
    sine[...] = jnp.where(lower, -turned, turned)

    tokens_copy.wait()
    pltpu.make_async_copy(w_key.at[:, columns], weight, sems.at[1]).wait()
    u = jnp.dot(tokens[...], weight[...], preferred_element_type=jnp.float32)

    @pl.when(core == 0)
    def _():
        out[...] = norm_rotate(u, gain[...], cosine[...], sine[...]).astype(out.dtype)

    @pl.when(core != 0)
    def _():
        out[...] = u.astype(out.dtype)


def project_kv(tokens, w_key, w_value, gain, lengths, heads):
    rows, width = tokens.shape
    frequency = jnp.asarray(np.tile(FREQUENCY, 2)[None], jnp.float32)
    table = jax.ShapeDtypeStruct((rows, HD), jnp.float32)
    return pl.pallas_call(
        functools.partial(kv_body, heads),
        out_shape=(
            jax.ShapeDtypeStruct((rows, HD), jnp.bfloat16),
            table,
            table,
            jax.ShapeDtypeStruct((rows, 1), jnp.int32),
            jax.ShapeDtypeStruct((2,), jnp.int32),
        ),
        in_specs=[pl.BlockSpec(memory_space=pltpu.HBM)] * 3
        + [pl.BlockSpec(memory_space=VMEM)] * 3,
        out_specs=(pl.BlockSpec(memory_space=VMEM),) * 4
        + (pl.BlockSpec(memory_space=pltpu.SMEM),),
        scratch_shapes=[
            VMEM((rows, width), tokens.dtype),
            VMEM((width, HD), w_key.dtype),
            pltpu.SemaphoreType.DMA((2,)),
        ],
        cost_estimate=pl.CostEstimate(
            flops=2 * rows * width * HD, bytes_accessed=4 * rows * width, transcendentals=0
        ),
        compiler_params=pltpu.CompilerParams(vmem_limit_bytes=63 << 20),
        name="project_kv",
    )(tokens, w_key, w_value, gain, lengths, frequency)


def q_body(heads, tokens, w_query, gain, cosine, sine, out):
    u = jnp.dot(tokens[...], w_query[...], preferred_element_type=jnp.float32)
    for h in range(heads):
        part = u[:, h * HD : (h + 1) * HD]
        out[h] = norm_rotate(part, gain[...], cosine[...], sine[...]).astype(out.dtype)


def project_q(tokens, w_query, gain, cosine, sine):
    rows, width = tokens.shape
    heads = w_query.shape[1] // HD
    return pl.pallas_call(
        functools.partial(q_body, heads),
        out_shape=jax.ShapeDtypeStruct((heads, rows, HD), jnp.bfloat16),
        in_specs=[pl.BlockSpec(memory_space=VMEM)] * 5,
        out_specs=pl.BlockSpec(memory_space=VMEM),
        cost_estimate=pl.CostEstimate(
            flops=2 * rows * width * heads * HD, bytes_accessed=6 * rows * width, transcendentals=0
        ),
        compiler_params=pltpu.CompilerParams(vmem_limit_bytes=10 << 20),
        name="project_q",
    )(tokens, w_query, gain, cosine, sine)


def add_block(heads, queries, key, value, total, weighted, mask):
    for h in range(heads):
        scores = lax.dot_general(
            queries[h], key, (((1,), (1,)), ((), ())), preferred_element_type=jnp.float32
        )
        weights = jnp.exp2(scores * (HD**-0.5 * LOG2E))
        if mask is not None:
            weights = weights * mask[...]
        total[h] += weights[:, :HD] + weights[:, HD:]
        weighted[h] += jnp.dot(
            weights.astype(jnp.bfloat16), value, preferred_element_type=jnp.float32
        )


def add_blocks(heads, distance_of, places, span, queries, starts, kv, total, weighted, mask):
    rows = queries.shape[1]
    block = lax.axis_index("ctx")
    first = span[0] // rows
    last = span[1]

    def step(place, carry):
        b = block - distance_of(place)

        @pl.when(b >= first)
        def _():
            key, value = kv[0, place], kv[1, place]
            whole = (b < block) & (b * rows >= last)

            @pl.when(whole)
            def _():
                add_block(heads, queries, key, value, total, weighted, None)

            @pl.when(jnp.logical_not(whole))
            def _():
                key_pos = b * rows + iota((rows, rows), 1)
                query_pos = block * rows + iota((rows, rows), 0)
                visible = (key_pos <= query_pos) & (key_pos >= starts[...])
                mask[...] = jnp.where(visible, 1.0, 0.0)
                add_block(heads, queries, key, value, total, weighted, mask)

        return carry

    lax.fori_loop(0, places, step, 0)


def start_copies(mine, theirs, kv, sems):
    core = lax.axis_index("c")
    copies = []
    for side, group in ((core, mine), (1 - core, theirs)):
        at = 0
        for ref in group:
            count = ref.shape[0]
            copies.append(
                pltpu.make_async_copy(
                    ref, kv.at[side, pl.ds(at, count)], sems.at[len(copies)]
                )
            )
            at += count
    for copy in copies:
        copy.start()
    return copies


def near_body(heads, n, span, queries, starts, *refs):
    mine, theirs = refs[:n], refs[n : 2 * n]
    total, weighted, mask, kv, sems = refs[2 * n :]
    copies = start_copies(mine, theirs, kv, sems)
    total[...] = jnp.zeros_like(total)
    weighted[...] = jnp.zeros_like(weighted)
    for copy in copies:
        copy.wait()

    def distance_of(place):
        return jnp.where(
            place == 0, 0, 1 + (place - 1) // LINE + LINE * ((place - 1 + LINE) % LINE)
        )

    add_blocks(
        heads, distance_of, kv.shape[1], span, queries, starts, kv, total, weighted, mask
    )


def attend_near(span, queries, starts, mine, theirs):
    heads, rows, _ = queries.shape
    n = len(mine)
    places = sum(a.shape[0] for a in mine)
    state = jax.ShapeDtypeStruct((heads, rows, HD), jnp.float32)
    return pl.pallas_call(
        functools.partial(near_body, heads, n),
        out_shape=(state, state),
        in_specs=[pl.BlockSpec(memory_space=pltpu.SMEM)]
        + [pl.BlockSpec(memory_space=VMEM)] * 2
        + [pl.BlockSpec(memory_space=pl.ANY)] * (2 * n),
        out_specs=(pl.BlockSpec(memory_space=VMEM),) * 2,
        scratch_shapes=[
            VMEM((rows, rows), jnp.float32),
            VMEM((2, places, rows, HD), jnp.bfloat16),
            pltpu.SemaphoreType.DMA((2 * n,)),
        ],
        cost_estimate=pl.CostEstimate(
            flops=16 * places * heads * rows * rows * HD, bytes_accessed=2 << 20, transcendentals=0
        ),
        compiler_params=pltpu.CompilerParams(vmem_limit_bytes=12 << 20),
        name="attend_near",
    )(span, queries, starts, *mine, *theirs)


def far_body(heads, n, span, queries, starts, total_in, weighted_in, *refs):
    mine, theirs = refs[:n], refs[n : 2 * n]
    w_out_any, keep, give, total, weighted, mask, attended, kv, w_out, sems = refs[2 * n :]
    copies = start_copies(mine, theirs, kv, sems)
    weights_copy = pltpu.make_async_copy(w_out_any, w_out, sems.at[2 * n])
    weights_copy.start()
    core = lax.axis_index("c")
    total[...] = total_in[...]
    weighted[...] = weighted_in[...]
    for copy in copies:
        copy.wait()

    def distance_of(place):
        return LINE - n + 1 + place // LINE + LINE * (place % LINE)

    add_blocks(
        heads, distance_of, kv.shape[1], span, queries, starts, kv, total, weighted, mask
    )
    for h in range(heads):
        sums = jnp.sum(total[h], axis=1, keepdims=True)
        attended[:, h * HD : (h + 1) * HD] = (weighted[h] / sums).astype(attended.dtype)
    weights_copy.wait()
    width = keep.shape[2]
    for out, side in ((give, 1 - core), (keep, core)):
        for x in range(keep.shape[0]):
            columns = pl.ds(pl.multiple_of((2 * x + side) * width, width), width)
            out[x] = jnp.dot(
                attended[...], w_out[:, columns], preferred_element_type=jnp.float32
            ).astype(out.dtype)


def attend_far(span, queries, starts, total, weighted, mine, theirs, w_out, chips):
    heads, rows, _ = queries.shape
    n = len(mine)
    places = sum(a.shape[0] for a in mine)
    width = w_out.shape[1] // (2 * chips)
    half = jax.ShapeDtypeStruct((chips, rows, width), jnp.bfloat16)
    return pl.pallas_call(
        functools.partial(far_body, heads, n),
        out_shape=(half, half),
        in_specs=[pl.BlockSpec(memory_space=pltpu.SMEM)]
        + [pl.BlockSpec(memory_space=VMEM)] * 4
        + [pl.BlockSpec(memory_space=pl.ANY)] * (2 * n + 1),
        out_specs=(pl.BlockSpec(memory_space=VMEM),) * 2,
        scratch_shapes=[
            VMEM((heads, rows, HD), jnp.float32),
            VMEM((heads, rows, HD), jnp.float32),
            VMEM((rows, rows), jnp.float32),
            VMEM((rows, heads * HD), jnp.bfloat16),
            VMEM((2, places, rows, HD), jnp.bfloat16),
            VMEM(w_out.shape, jnp.bfloat16),
            pltpu.SemaphoreType.DMA((2 * n + 1,)),
        ],
        cost_estimate=pl.CostEstimate(
            flops=4 * places * heads * rows * rows * HD, bytes_accessed=4 << 20, transcendentals=0
        ),
        compiler_params=pltpu.CompilerParams(vmem_limit_bytes=16 << 20),
        name="attend_far",
    )(span, queries, starts, total, weighted, *mine, *theirs, w_out)


def passed_along(a, distance):
    n = lax.axis_size("ctx")
    return lax.ppermute(a, "ctx", [(i, i + distance) for i in range(n - distance)])


def swapped(a):
    return lax.ppermute(a, "c", [(0, 1), (1, 0)])


def local(tokens, w_query, w_key, w_value, w_out, query_gain, key_gain, doc_lengths):
    heads = w_query.shape[1] // HD
    chips = lax.axis_size("x")
    part, cosine, sine, starts, span = project_kv(
        tokens, w_key, w_value, key_gain[None], doc_lengths[None], heads
    )
    own = part[None]
    far = [passed_along(part, LINE + 1)]
    far.append(passed_along(far[-1], LINE))
    queries = project_q(tokens, w_query, query_gain[None], cosine, sine)
    middle, queries = lax.optimization_barrier((far[-1], queries))
    far.append(passed_along(middle, LINE))
    hops = [jnp.stack([passed_along(part, 1)] + far)]
    theirs = [swapped(own)]
    for _ in range(LINE - 1):
        hop, theirs = lax.optimization_barrier((hops[-1], theirs))
        hops.append(passed_along(hop, 1))
        theirs = theirs + [swapped(hop)]
    mine = [own] + hops

    state = attend_near(span, queries, starts, mine[:3], theirs[:3])
    last, (total, weighted) = lax.optimization_barrier((hops[-1], state))
    theirs.append(swapped(last))
    keep, give = attend_far(
        span, queries, starts, total, weighted, mine[3:], theirs[3:], w_out, chips
    )
    pairs = (keep.astype(jnp.float32) + swapped(give).astype(jnp.float32)).astype(jnp.bfloat16)
    terms = lax.all_to_all(pairs, "x", 0, 0, tiled=True)
    return jnp.sum(terms.astype(jnp.float32), axis=0).astype(jnp.bfloat16)


def solution(mesh):
    ctx, tp = mesh.shape["ctx"], mesh.shape["tp"]
    fine = Mesh(mesh.devices.reshape(ctx, tp // 2, 2), ("ctx",) + TP)
    return jax.shard_map(
        local,
        mesh=fine,
        in_specs=(P("ctx", None), P(None, TP), P(), P(), P(TP, None), P(), P(), P()),
        out_specs=P("ctx", TP),
        check_vma=False,
    )
```

```python
import functools

import jax
import jax.numpy as jnp
import numpy as np
from jax import lax
from jax.experimental import pallas as pl
from jax.experimental.pallas import tpu as pltpu
from jax.sharding import Mesh, PartitionSpec as P


H = 32
KVH = 4
HD = 128
LINE = 4
EPSILON = 1e-06
ROPE_BASE = 1000000.0
LOG2E = 1.4426950408889634

TP = ("x", "c")
VMEM = pltpu.VMEM
FREQUENCY = ROPE_BASE ** (-2.0 * np.arange(HD // 2, dtype=np.float64) / HD)


def norm_rotate(u, gain, cosine, sine):
    inv = lax.rsqrt(jnp.mean(u * u, axis=-1, keepdims=True) + EPSILON)
    w = u * inv * gain
    return w * cosine + pltpu.roll(w, HD // 2, 1) * sine


def iota(shape, axis):
    return lax.broadcasted_iota(jnp.int32, shape, axis)


def kv_body(
    heads, tokens_hbm, w_key, w_value, gain, lengths, frequency,
    out, cosine, sine, starts, span, tokens, weight, sems,
):
    rows = out.shape[0]
    docs = lengths.shape[1]
    core = lax.axis_index("c")
    block = lax.axis_index("ctx")
    head = (2 * lax.axis_index("x") + core) * heads // (H // KVH)
    columns = pl.ds(pl.multiple_of(head * HD, HD), HD)
    tokens_copy = pltpu.make_async_copy(tokens_hbm, tokens, sems.at[0])
    tokens_copy.start()

    @pl.when(core == 0)
    def _():
        pltpu.make_async_copy(w_key.at[:, columns], weight, sems.at[1]).start()

    @pl.when(core != 0)
    def _():
        pltpu.make_async_copy(w_value.at[:, columns], weight, sems.at[1]).start()

    counts = lengths[...].astype(jnp.float32)
    before = iota((docs, docs), 1) <= iota((docs, docs), 0)
    ends = jnp.sum(jnp.where(before, counts, 0.0), axis=1, keepdims=True)
    here = (block * rows + iota((docs, rows), 1)).astype(jnp.float32)
    start_row = jnp.max(jnp.where(ends <= here, ends, 0.0), axis=0, keepdims=True)
    same = iota((rows, rows), 0) == iota((rows, rows), 1)
    start_column = jnp.sum(jnp.where(same, start_row, 0.0), axis=1, keepdims=True)
    starts[...] = start_column.astype(jnp.int32)
    span[0] = jnp.min(start_row).astype(jnp.int32)
    span[1] = jnp.max(start_row).astype(jnp.int32)
    offsets = (block * rows + iota((rows, 1), 0)).astype(jnp.float32) - start_column
    half = rows // 2
    lower = iota((half, HD), 1) < HD // 2
    angles = jnp.where(lower, offsets[:half], offsets[half:]) * frequency[...]
    for table, wave in ((cosine, jnp.cos(angles)), (sine, jnp.sin(angles))):
        other = pltpu.roll(wave, HD // 2, 1)
        sign = -1.0 if table is sine else 1.0
        table[:half] = jnp.where(lower, sign * wave, other)
        table[half:] = jnp.where(lower, sign * other, wave)

    tokens_copy.wait()
    pltpu.make_async_copy(w_key.at[:, columns], weight, sems.at[1]).wait()
    u = jnp.dot(tokens[...], weight[...], preferred_element_type=jnp.float32)

    @pl.when(core == 0)
    def _():
        out[...] = norm_rotate(u, gain[...], cosine[...], sine[...]).astype(out.dtype)

    @pl.when(core != 0)
    def _():
        out[...] = u.astype(out.dtype)


def project_kv(tokens, w_key, w_value, gain, lengths, heads):
    rows, width = tokens.shape
    frequency = jnp.asarray(np.tile(FREQUENCY, 2)[None], jnp.float32)
    table = jax.ShapeDtypeStruct((rows, HD), jnp.float32)
    return pl.pallas_call(
        functools.partial(kv_body, heads),
        out_shape=(
            jax.ShapeDtypeStruct((rows, HD), jnp.bfloat16),
            table,
            table,
            jax.ShapeDtypeStruct((rows, 1), jnp.int32),
            jax.ShapeDtypeStruct((2,), jnp.int32),
        ),
        in_specs=[pl.BlockSpec(memory_space=pltpu.HBM)] * 3
        + [pl.BlockSpec(memory_space=VMEM)] * 3,
        out_specs=(pl.BlockSpec(memory_space=VMEM),) * 4
        + (pl.BlockSpec(memory_space=pltpu.SMEM),),
        scratch_shapes=[
            VMEM((rows, width), tokens.dtype),
            VMEM((width, HD), w_key.dtype),
            pltpu.SemaphoreType.DMA((2,)),
        ],
        cost_estimate=pl.CostEstimate(
            flops=2 * rows * width * HD, bytes_accessed=4 * rows * width, transcendentals=0
        ),
        compiler_params=pltpu.CompilerParams(vmem_limit_bytes=63 << 20),
        name="project_kv",
    )(tokens, w_key, w_value, gain, lengths, frequency)


def q_body(tokens_hbm, w_hbm, gain, cosine_any, sine_any, out, tokens, weight, cosine, sine, sems):
    wide = weight.shape[2]
    copies = [
        pltpu.make_async_copy(tokens_hbm, tokens, sems.at[0]),
        pltpu.make_async_copy(w_hbm.at[:, pl.ds(0, wide)], weight.at[0], sems.at[1]),
        pltpu.make_async_copy(cosine_any, cosine, sems.at[2]),
        pltpu.make_async_copy(sine_any, sine, sems.at[3]),
    ]
    later = []
    for i in range(1, weight.shape[0]):
        later.append(
            pltpu.make_async_copy(
                w_hbm.at[:, pl.ds(i * wide, wide)], weight.at[i], sems.at[3 + i]
            )
        )
    for copy in copies + later:
        copy.start()
    for copy in copies:
        copy.wait()
    each = wide // HD
    for i in range(weight.shape[0]):
        if i > 0:
            later[i - 1].wait()
        u = jnp.dot(tokens[...], weight[i], preferred_element_type=jnp.float32)
        for h in range(each):
            part = u[:, h * HD : (h + 1) * HD]
            turned = norm_rotate(part, gain[...], cosine[...], sine[...])
            out[i * each + h] = turned.astype(out.dtype)


def project_q(tokens, w_query, gain, cosine, sine):
    rows, width = tokens.shape
    heads = w_query.shape[1] // HD
    chunks = 2
    return pl.pallas_call(
        q_body,
        out_shape=jax.ShapeDtypeStruct((heads, rows, HD), jnp.bfloat16),
        in_specs=[pl.BlockSpec(memory_space=pltpu.HBM)] * 2
        + [pl.BlockSpec(memory_space=VMEM)]
        + [pl.BlockSpec(memory_space=pl.ANY)] * 2,
        out_specs=pl.BlockSpec(memory_space=VMEM),
        scratch_shapes=[
            VMEM((rows, width), tokens.dtype),
            VMEM((chunks, width, heads * HD // chunks), w_query.dtype),
            VMEM((rows, HD), jnp.float32),
            VMEM((rows, HD), jnp.float32),
            pltpu.SemaphoreType.DMA((3 + chunks,)),
        ],
        cost_estimate=pl.CostEstimate(
            flops=2 * rows * width * heads * HD, bytes_accessed=6 * rows * width, transcendentals=0
        ),
        compiler_params=pltpu.CompilerParams(vmem_limit_bytes=63 << 20),
        name="project_q",
    )(tokens, w_query, gain, cosine, sine)


def add_block(heads, queries, key, value, total, weighted, mask):
    for h in range(heads):
        scores = lax.dot_general(
            queries[h], key, (((1,), (1,)), ((), ())), preferred_element_type=jnp.float32
        )
        weights = jnp.exp2(scores * (HD**-0.5 * LOG2E))
        if mask is not None:
            weights = weights * mask[...]
        total[h] += weights[:, :HD] + weights[:, HD:]
        weighted[h] += jnp.dot(
            weights.astype(jnp.bfloat16), value, preferred_element_type=jnp.float32
        )


def add_blocks(heads, distance_of, places, span, queries, starts, kv, total, weighted, mask):
    rows = queries.shape[1]
    block = lax.axis_index("ctx")
    first = span[0] // rows
    last = span[1]

    def step(place, carry):
        b = block - distance_of(place)

        @pl.when(b >= first)
        def _():
            key, value = kv[0, place], kv[1, place]
            whole = (b < block) & (b * rows >= last)

            @pl.when(whole)
            def _():
                add_block(heads, queries, key, value, total, weighted, None)

            @pl.when(jnp.logical_not(whole))
            def _():
                key_pos = b * rows + iota((rows, rows), 1)
                query_pos = block * rows + iota((rows, rows), 0)
                visible = (key_pos <= query_pos) & (key_pos >= starts[...])
                mask[...] = jnp.where(visible, 1.0, 0.0)
                add_block(heads, queries, key, value, total, weighted, mask)

        return carry

    lax.fori_loop(0, places, step, 0)


def start_copies(mine, theirs, kv, sems):
    core = lax.axis_index("c")
    copies = []
    for side, group in ((core, mine), (1 - core, theirs)):
        at = 0
        for ref in group:
            count = ref.shape[0]
            copies.append(
                pltpu.make_async_copy(
                    ref, kv.at[side, pl.ds(at, count)], sems.at[len(copies)]
                )
            )
            at += count
    for copy in copies:
        copy.start()
    return copies


def near_body(heads, n, span, queries, starts, *refs):
    mine, theirs = refs[:n], refs[n : 2 * n]
    total, weighted, mask, kv, sems = refs[2 * n :]
    copies = start_copies(mine, theirs, kv, sems)
    total[...] = jnp.zeros_like(total)
    weighted[...] = jnp.zeros_like(weighted)
    for copy in copies:
        copy.wait()

    def distance_of(place):
        return jnp.where(
            place == 0, 0, 1 + (place - 1) // LINE + LINE * ((place - 1 + LINE) % LINE)
        )

    add_blocks(
        heads, distance_of, kv.shape[1], span, queries, starts, kv, total, weighted, mask
    )


def attend_near(span, queries, starts, mine, theirs):
    heads, rows, _ = queries.shape
    n = len(mine)
    places = sum(a.shape[0] for a in mine)
    state = jax.ShapeDtypeStruct((heads, rows, HD), jnp.float32)
    return pl.pallas_call(
        functools.partial(near_body, heads, n),
        out_shape=(state, state),
        in_specs=[pl.BlockSpec(memory_space=pltpu.SMEM)]
        + [pl.BlockSpec(memory_space=VMEM)] * 2
        + [pl.BlockSpec(memory_space=pl.ANY)] * (2 * n),
        out_specs=(pl.BlockSpec(memory_space=VMEM),) * 2,
        scratch_shapes=[
            VMEM((rows, rows), jnp.float32),
            VMEM((2, places, rows, HD), jnp.bfloat16),
            pltpu.SemaphoreType.DMA((2 * n,)),
        ],
        cost_estimate=pl.CostEstimate(
            flops=16 * places * heads * rows * rows * HD, bytes_accessed=2 << 20, transcendentals=0
        ),
        compiler_params=pltpu.CompilerParams(vmem_limit_bytes=12 << 20),
        name="attend_near",
    )(span, queries, starts, *mine, *theirs)


def far_body(heads, n, span, queries, starts, total_in, weighted_in, *refs):
    mine, theirs = refs[:n], refs[n : 2 * n]
    w_out_any, keep, give, total, weighted, mask, attended, kv, w_out, sems = refs[2 * n :]
    copies = start_copies(mine, theirs, kv, sems)
    weights_copy = pltpu.make_async_copy(w_out_any, w_out, sems.at[2 * n])
    weights_copy.start()
    core = lax.axis_index("c")
    total[...] = total_in[...]
    weighted[...] = weighted_in[...]
    for copy in copies:
        copy.wait()

    def distance_of(place):
        return LINE - n + 1 + place // LINE + LINE * (place % LINE)

    add_blocks(
        heads, distance_of, kv.shape[1], span, queries, starts, kv, total, weighted, mask
    )
    for h in range(heads):
        sums = jnp.sum(total[h], axis=1, keepdims=True)
        attended[:, h * HD : (h + 1) * HD] = (weighted[h] / sums).astype(attended.dtype)
    weights_copy.wait()
    width = keep.shape[2]
    for out, side in ((give, 1 - core), (keep, core)):
        for x in range(keep.shape[0]):
            columns = pl.ds(pl.multiple_of((2 * x + side) * width, width), width)
            out[x] = jnp.dot(
                attended[...], w_out[:, columns], preferred_element_type=jnp.float32
            ).astype(out.dtype)


def attend_far(span, queries, starts, total, weighted, mine, theirs, w_out, chips):
    heads, rows, _ = queries.shape
    n = len(mine)
    places = sum(a.shape[0] for a in mine)
    width = w_out.shape[1] // (2 * chips)
    half = jax.ShapeDtypeStruct((chips, rows, width), jnp.bfloat16)
    return pl.pallas_call(
        functools.partial(far_body, heads, n),
        out_shape=(half, half),
        in_specs=[pl.BlockSpec(memory_space=pltpu.SMEM)]
        + [pl.BlockSpec(memory_space=VMEM)] * 4
        + [pl.BlockSpec(memory_space=pl.ANY)] * (2 * n + 1),
        out_specs=(pl.BlockSpec(memory_space=VMEM),) * 2,
        scratch_shapes=[
            VMEM((heads, rows, HD), jnp.float32),
            VMEM((heads, rows, HD), jnp.float32),
            VMEM((rows, rows), jnp.float32),
            VMEM((rows, heads * HD), jnp.bfloat16),
            VMEM((2, places, rows, HD), jnp.bfloat16),
            VMEM(w_out.shape, jnp.bfloat16),
            pltpu.SemaphoreType.DMA((2 * n + 1,)),
        ],
        cost_estimate=pl.CostEstimate(
            flops=4 * places * heads * rows * rows * HD, bytes_accessed=4 << 20, transcendentals=0
        ),
        compiler_params=pltpu.CompilerParams(vmem_limit_bytes=16 << 20),
        name="attend_far",
    )(span, queries, starts, total, weighted, *mine, *theirs, w_out)


def passed_along(a, distance):
    n = lax.axis_size("ctx")
    return lax.ppermute(a, "ctx", [(i, i + distance) for i in range(n - distance)])


def swapped(a):
    return lax.ppermute(a, "c", [(0, 1), (1, 0)])


def local(tokens, w_query, w_key, w_value, w_out, query_gain, key_gain, doc_lengths):
    heads = w_query.shape[1] // HD
    chips = lax.axis_size("x")
    part, cosine, sine, starts, span = project_kv(
        tokens, w_key, w_value, key_gain[None], doc_lengths[None], heads
    )
    own = part[None]
    far = [passed_along(part, LINE + 1)]
    near = passed_along(part, 1)
    theirs = [swapped(own)]
    for _ in range(2):
        far.append(passed_along(far[-1], LINE))
    queries = project_q(tokens, w_query, query_gain[None], cosine, sine)
    hops = [jnp.stack([near] + far)]
    for _ in range(LINE - 1):
        hops.append(passed_along(hops[-1], 1))
        theirs = theirs + [swapped(hops[-2])]
    mine = [own] + hops
    total, weighted = attend_near(span, queries, starts, mine[:3], theirs[:3])
    theirs.append(swapped(hops[-1]))
    keep, give = attend_far(
        span, queries, starts, total, weighted, mine[3:], theirs[3:], w_out, chips
    )
    pairs = (keep.astype(jnp.float32) + swapped(give).astype(jnp.float32)).astype(jnp.bfloat16)
    terms = lax.all_to_all(pairs, "x", 0, 0, tiled=True)
    return jnp.sum(terms.astype(jnp.float32), axis=0).astype(jnp.bfloat16)


def solution(mesh):
    ctx, tp = mesh.shape["ctx"], mesh.shape["tp"]
    fine = Mesh(mesh.devices.reshape(ctx, tp // 2, 2), ("ctx",) + TP)
    return jax.shard_map(
        local,
        mesh=fine,
        in_specs=(P("ctx", None), P(None, TP), P(), P(), P(TP, None), P(), P(), P()),
        out_specs=P("ctx", TP),
        check_vma=False,
    )
```

```python
import functools

import jax
import jax.numpy as jnp
import numpy as np
from jax import lax
from jax.experimental import pallas as pl
from jax.experimental.pallas import tpu as pltpu
from jax.sharding import Mesh, PartitionSpec as P


H = 32
KVH = 4
HD = 128
LINE = 4
EPSILON = 1e-06
ROPE_BASE = 1000000.0
LOG2E = 1.4426950408889634

TP = ("x", "c")
VMEM = pltpu.VMEM
FREQUENCY = ROPE_BASE ** (-2.0 * np.arange(HD // 2, dtype=np.float64) / HD)


def norm_rotate(u, gain, cosine, sine):
    inv = lax.rsqrt(jnp.mean(u * u, axis=-1, keepdims=True) + EPSILON)
    w = u * inv * gain
    return w * cosine + pltpu.roll(w, HD // 2, 1) * sine


def iota(shape, axis):
    return lax.broadcasted_iota(jnp.int32, shape, axis)


def kv_body(
    heads, tokens_hbm, w_key, w_value, gain, lengths, frequency,
    out, cosine, sine, starts, span, tokens, weight, sems,
):
    rows = out.shape[0]
    docs = lengths.shape[1]
    core = lax.axis_index("c")
    block = lax.axis_index("ctx")
    head = (2 * lax.axis_index("x") + core) * heads // (H // KVH)
    columns = pl.ds(pl.multiple_of(head * HD, HD), HD)
    tokens_copy = pltpu.make_async_copy(tokens_hbm, tokens, sems.at[0])
    tokens_copy.start()

    @pl.when(core == 0)
    def _():
        pltpu.make_async_copy(w_key.at[:, columns], weight, sems.at[1]).start()

    @pl.when(core != 0)
    def _():
        pltpu.make_async_copy(w_value.at[:, columns], weight, sems.at[1]).start()

    counts = lengths[...].astype(jnp.float32)
    before = iota((docs, docs), 1) <= iota((docs, docs), 0)
    ends = jnp.sum(jnp.where(before, counts, 0.0), axis=1, keepdims=True)
    here = (block * rows + iota((docs, rows), 1)).astype(jnp.float32)
    start_row = jnp.max(jnp.where(ends <= here, ends, 0.0), axis=0, keepdims=True)
    same = iota((rows, rows), 0) == iota((rows, rows), 1)
    start_column = jnp.sum(jnp.where(same, start_row, 0.0), axis=1, keepdims=True)
    starts[...] = start_column.astype(jnp.int32)
    span[0] = jnp.min(start_row).astype(jnp.int32)
    span[1] = jnp.max(start_row).astype(jnp.int32)
    offsets = (block * rows + iota((rows, 1), 0)).astype(jnp.float32) - start_column
    half = rows // 2
    lower = iota((half, HD), 1) < HD // 2
    angles = jnp.where(lower, offsets[:half], offsets[half:]) * frequency[...]
    for table, wave in ((cosine, jnp.cos(angles)), (sine, jnp.sin(angles))):
        other = pltpu.roll(wave, HD // 2, 1)
        sign = -1.0 if table is sine else 1.0
        table[:half] = jnp.where(lower, sign * wave, other)
        table[half:] = jnp.where(lower, sign * other, wave)

    tokens_copy.wait()
    pltpu.make_async_copy(w_key.at[:, columns], weight, sems.at[1]).wait()
    u = jnp.dot(tokens[...], weight[...], preferred_element_type=jnp.float32)

    @pl.when(core == 0)
    def _():
        out[...] = norm_rotate(u, gain[...], cosine[...], sine[...]).astype(out.dtype)

    @pl.when(core != 0)
    def _():
        out[...] = u.astype(out.dtype)


def project_kv(tokens, w_key, w_value, gain, lengths, heads):
    rows, width = tokens.shape
    frequency = jnp.asarray(np.tile(FREQUENCY, 2)[None], jnp.float32)
    table = jax.ShapeDtypeStruct((rows, HD), jnp.float32)
    return pl.pallas_call(
        functools.partial(kv_body, heads),
        out_shape=(
            jax.ShapeDtypeStruct((rows, HD), jnp.bfloat16),
            table,
            table,
            jax.ShapeDtypeStruct((rows, 1), jnp.int32),
            jax.ShapeDtypeStruct((2,), jnp.int32),
        ),
        in_specs=[pl.BlockSpec(memory_space=pltpu.HBM)] * 3
        + [pl.BlockSpec(memory_space=VMEM)] * 3,
        out_specs=(pl.BlockSpec(memory_space=VMEM),) * 4
        + (pl.BlockSpec(memory_space=pltpu.SMEM),),
        scratch_shapes=[
            VMEM((rows, width), tokens.dtype),
            VMEM((width, HD), w_key.dtype),
            pltpu.SemaphoreType.DMA((2,)),
        ],
        cost_estimate=pl.CostEstimate(
            flops=2 * rows * width * HD, bytes_accessed=4 * rows * width, transcendentals=0
        ),
        compiler_params=pltpu.CompilerParams(vmem_limit_bytes=63 << 20),
        name="project_kv",
    )(tokens, w_key, w_value, gain, lengths, frequency)


def q_body(tokens_hbm, w_hbm, gain, cosine_any, sine_any, out, tokens, weight, cosine, sine, sems):
    wide = weight.shape[2]
    copies = [
        pltpu.make_async_copy(tokens_hbm, tokens, sems.at[0]),
        pltpu.make_async_copy(w_hbm.at[:, pl.ds(0, wide)], weight.at[0], sems.at[1]),
        pltpu.make_async_copy(cosine_any, cosine, sems.at[2]),
        pltpu.make_async_copy(sine_any, sine, sems.at[3]),
    ]
    later = []
    for i in range(1, weight.shape[0]):
        later.append(
            pltpu.make_async_copy(
                w_hbm.at[:, pl.ds(i * wide, wide)], weight.at[i], sems.at[3 + i]
            )
        )
    for copy in copies + later:
        copy.start()
    for copy in copies:
        copy.wait()
    each = wide // HD
    for i in range(weight.shape[0]):
        if i > 0:
            later[i - 1].wait()
        u = jnp.dot(tokens[...], weight[i], preferred_element_type=jnp.float32)
        for h in range(each):
            part = u[:, h * HD : (h + 1) * HD]
            turned = norm_rotate(part, gain[...], cosine[...], sine[...])
            out[i * each + h] = turned.astype(out.dtype)


def project_q(tokens, w_query, gain, cosine, sine):
    rows, width = tokens.shape
    heads = w_query.shape[1] // HD
    chunks = 2
    return pl.pallas_call(
        q_body,
        out_shape=jax.ShapeDtypeStruct((heads, rows, HD), jnp.bfloat16),
        in_specs=[pl.BlockSpec(memory_space=pltpu.HBM)] * 2
        + [pl.BlockSpec(memory_space=VMEM)]
        + [pl.BlockSpec(memory_space=pl.ANY)] * 2,
        out_specs=pl.BlockSpec(memory_space=VMEM),
        scratch_shapes=[
            VMEM((rows, width), tokens.dtype),
            VMEM((chunks, width, heads * HD // chunks), w_query.dtype),
            VMEM((rows, HD), jnp.float32),
            VMEM((rows, HD), jnp.float32),
            pltpu.SemaphoreType.DMA((3 + chunks,)),
        ],
        cost_estimate=pl.CostEstimate(
            flops=2 * rows * width * heads * HD, bytes_accessed=6 * rows * width, transcendentals=0
        ),
        compiler_params=pltpu.CompilerParams(vmem_limit_bytes=63 << 20),
        name="project_q",
    )(tokens, w_query, gain, cosine, sine)


def scored(query, key):
    return lax.dot_general(
        query, key, (((1,), (1,)), ((), ())), preferred_element_type=jnp.float32
    )


def add_block(heads, queries, key, value, total, weighted, mask):
    scores = scored(queries[0], key)
    for h in range(heads):
        following = scored(queries[h + 1], key) if h + 1 < heads else None
        weights = jnp.exp2(scores * (HD**-0.5 * LOG2E))
        if mask is not None:
            weights = weights * mask[...]
        sums = weights[:, :HD]
        for at in range(HD, weights.shape[1], HD):
            sums = sums + weights[:, at : at + HD]
        total[h] += sums
        weighted[h] += jnp.dot(
            weights.astype(jnp.bfloat16), value, preferred_element_type=jnp.float32
        )
        scores = following


def add_blocks(heads, distance_of, deepest, span, queries, starts, kv, total, weighted, mask):
    rows = queries.shape[1]
    places = kv.shape[1]
    block = lax.axis_index("ctx")
    first = span[0] // rows
    last = span[1]

    def step(place, carry):
        b = block - distance_of(place)

        @pl.when(b >= first)
        def _():
            key, value = kv[0, place], kv[1, place]
            whole = (b < block) & (b * rows >= last)

            @pl.when(whole)
            def _():
                add_block(heads, queries, key, value, total, weighted, None)

            @pl.when(jnp.logical_not(whole))
            def _():
                key_pos = b * rows + iota((rows, rows), 1)
                query_pos = block * rows + iota((rows, rows), 0)
                visible = (key_pos <= query_pos) & (key_pos >= starts[...])
                mask[...] = jnp.where(visible, 1.0, 0.0)
                add_block(heads, queries, key, value, total, weighted, mask)

        return carry

    together = (block - deepest) * rows >= last

    @pl.when(together)
    def _():
        four = pl.ds(places - LINE, LINE)
        key = kv[0, four].reshape(LINE * rows, HD)
        value = kv[1, four].reshape(LINE * rows, HD)
        add_block(heads, queries, key, value, total, weighted, None)

    lax.fori_loop(0, jnp.where(together, places - LINE, places), step, 0)


def start_copies(mine, theirs, kv, sems):
    core = lax.axis_index("c")
    copies = []
    for side, group in ((core, mine), (1 - core, theirs)):
        at = 0
        for ref in group:
            count = ref.shape[0]
            copies.append(
                pltpu.make_async_copy(
                    ref, kv.at[side, pl.ds(at, count)], sems.at[len(copies)]
                )
            )
            at += count
    for copy in copies:
        copy.start()
    return copies


def near_body(heads, first_call, distance_of, deepest, n, span, queries, starts, *refs):
    if not first_call:
        total_in, weighted_in, refs = refs[0], refs[1], refs[2:]
    mine, theirs = refs[:n], refs[n : 2 * n]
    total, weighted, mask, kv, sems = refs[2 * n :]
    copies = start_copies(mine, theirs, kv, sems)
    if first_call:
        total[...] = jnp.zeros_like(total)
        weighted[...] = jnp.zeros_like(weighted)
    else:
        total[...] = total_in[...]
        weighted[...] = weighted_in[...]
    for copy in copies:
        copy.wait()
    add_blocks(
        heads, distance_of, deepest, span, queries, starts, kv, total, weighted, mask
    )


def attend_near(span, queries, starts, state, mine, theirs, distance_of, deepest):
    heads, rows, _ = queries.shape
    n = len(mine)
    places = sum(a.shape[0] for a in mine)
    shape = jax.ShapeDtypeStruct((heads, rows, HD), jnp.float32)
    return pl.pallas_call(
        functools.partial(near_body, heads, not state, distance_of, deepest, n),
        out_shape=(shape, shape),
        in_specs=[pl.BlockSpec(memory_space=pltpu.SMEM)]
        + [pl.BlockSpec(memory_space=VMEM)] * (2 + len(state))
        + [pl.BlockSpec(memory_space=pl.ANY)] * (2 * n),
        out_specs=(pl.BlockSpec(memory_space=VMEM),) * 2,
        scratch_shapes=[
            VMEM((rows, rows), jnp.float32),
            VMEM((2, places, rows, HD), jnp.bfloat16),
            pltpu.SemaphoreType.DMA((2 * n,)),
        ],
        cost_estimate=pl.CostEstimate(
            flops=4 * places * heads * rows * rows * HD, bytes_accessed=2 << 20, transcendentals=0
        ),
        compiler_params=pltpu.CompilerParams(vmem_limit_bytes=12 << 20),
    )(span, queries, starts, *state, *mine, *theirs)


def far_body(heads, n, span, queries, starts, total_in, weighted_in, *refs):
    mine, theirs = refs[:n], refs[n : 2 * n]
    w_out_any, keep, give, total, weighted, mask, attended, kv, w_out, sems = refs[2 * n :]
    copies = start_copies(mine, theirs, kv, sems)
    weights_copy = pltpu.make_async_copy(w_out_any, w_out, sems.at[2 * n])
    weights_copy.start()
    core = lax.axis_index("c")
    total[...] = total_in[...]
    weighted[...] = weighted_in[...]
    for copy in copies:
        copy.wait()

    deepest = LINE * LINE

    def distance_of(place):
        return LINE + LINE * place

    add_blocks(
        heads, distance_of, deepest, span, queries, starts, kv, total, weighted, mask
    )
    for h in range(heads):
        sums = jnp.sum(total[h], axis=1, keepdims=True)
        attended[:, h * HD : (h + 1) * HD] = (weighted[h] / sums).astype(attended.dtype)
    weights_copy.wait()
    width = keep.shape[2]
    for out, side in ((give, 1 - core), (keep, core)):
        for x in range(keep.shape[0]):
            columns = pl.ds(pl.multiple_of((2 * x + side) * width, width), width)
            out[x] = jnp.dot(
                attended[...], w_out[:, columns], preferred_element_type=jnp.float32
            ).astype(out.dtype)


def attend_far(span, queries, starts, total, weighted, mine, theirs, w_out, chips):
    heads, rows, _ = queries.shape
    n = len(mine)
    places = sum(a.shape[0] for a in mine)
    width = w_out.shape[1] // (2 * chips)
    half = jax.ShapeDtypeStruct((chips, rows, width), jnp.bfloat16)
    return pl.pallas_call(
        functools.partial(far_body, heads, n),
        out_shape=(half, half),
        in_specs=[pl.BlockSpec(memory_space=pltpu.SMEM)]
        + [pl.BlockSpec(memory_space=VMEM)] * 4
        + [pl.BlockSpec(memory_space=pl.ANY)] * (2 * n + 1),
        out_specs=(pl.BlockSpec(memory_space=VMEM),) * 2,
        scratch_shapes=[
            VMEM((heads, rows, HD), jnp.float32),
            VMEM((heads, rows, HD), jnp.float32),
            VMEM((rows, rows), jnp.float32),
            VMEM((rows, heads * HD), jnp.bfloat16),
            VMEM((2, places, rows, HD), jnp.bfloat16),
            VMEM(w_out.shape, jnp.bfloat16),
            pltpu.SemaphoreType.DMA((2 * n + 1,)),
        ],
        cost_estimate=pl.CostEstimate(
            flops=4 * places * heads * rows * rows * HD, bytes_accessed=4 << 20, transcendentals=0
        ),
        compiler_params=pltpu.CompilerParams(vmem_limit_bytes=16 << 20),
        name="attend_far",
    )(span, queries, starts, total, weighted, *mine, *theirs, w_out)


def passed_along(a, distance):
    n = lax.axis_size("ctx")
    return lax.ppermute(a, "ctx", [(i, i + distance) for i in range(n - distance)])


def swapped(a):
    return lax.ppermute(a, "c", [(0, 1), (1, 0)])


def local(tokens, w_query, w_key, w_value, w_out, query_gain, key_gain, doc_lengths):
    heads = w_query.shape[1] // HD
    chips = lax.axis_size("x")
    part, cosine, sine, starts, span = project_kv(
        tokens, w_key, w_value, key_gain[None], doc_lengths[None], heads
    )
    own = part[None]
    far = [passed_along(part, LINE + 1)]
    near = passed_along(part, 1)
    theirs = [swapped(own)]
    for _ in range(2):
        far.append(passed_along(far[-1], LINE))
    queries = project_q(tokens, w_query, query_gain[None], cosine, sine)
    hops = [jnp.stack([near] + far)]
    for _ in range(LINE - 1):
        hops.append(passed_along(hops[-1], 1))
        theirs = theirs + [swapped(hops[-2])]
    mine = [own] + hops
    theirs.append(swapped(hops[-1]))
    state = ()
    for i, (low, high) in enumerate(((0, 2), (2, 3), (3, 4))):

        def distance_of(place, i=i):
            if i == 0:
                return jnp.where(place == 0, 0, 1 + LINE * (place - 1))
            return 1 + i + LINE * place

        state = attend_near(
            span, queries, starts, state, mine[low:high], theirs[low:high],
            distance_of, 1 + i + LINE * (LINE - 1),
        )
    total, weighted = state
    keep, give = attend_far(
        span, queries, starts, total, weighted, mine[4:], theirs[4:], w_out, chips
    )
    pairs = (keep.astype(jnp.float32) + swapped(give).astype(jnp.float32)).astype(jnp.bfloat16)
    terms = lax.all_to_all(pairs, "x", 0, 0, tiled=True)
    return jnp.sum(terms.astype(jnp.float32), axis=0).astype(jnp.bfloat16)


def solution(mesh):
    ctx, tp = mesh.shape["ctx"], mesh.shape["tp"]
    fine = Mesh(mesh.devices.reshape(ctx, tp // 2, 2), ("ctx",) + TP)
    return jax.shard_map(
        local,
        mesh=fine,
        in_specs=(P("ctx", None), P(None, TP), P(), P(), P(TP, None), P(), P(), P()),
        out_specs=P("ctx", TP),
        check_vma=False,
    )
```

```python
import functools

import jax
import jax.numpy as jnp
import numpy as np
from jax import lax
from jax.experimental import pallas as pl
from jax.experimental.pallas import tpu as pltpu
from jax.sharding import Mesh, PartitionSpec as P


H = 32
KVH = 4
HD = 128
REACH = 16
LINE = 4
EPSILON = 1e-06
ROPE_BASE = 1000000.0
LOG2E = 1.4426950408889634

TP = ("x", "c")
VMEM = pltpu.VMEM
FREQUENCY = ROPE_BASE ** (-2.0 * np.arange(HD // 2, dtype=np.float64) / HD)


def norm_rotate(u, gain, cosine, sine):
    inv = lax.rsqrt(jnp.mean(u * u, axis=-1, keepdims=True) + EPSILON)
    w = u * inv * gain
    return w * cosine + pltpu.roll(w, HD // 2, 1) * sine


def iota(shape, axis):
    return lax.broadcasted_iota(jnp.int32, shape, axis)


def kv_body(
    heads, tokens_hbm, w_key, w_value, gain, lengths, frequency,
    out, cosine, sine, starts, span, tokens, weight, sems,
):
    rows = out.shape[0]
    docs = lengths.shape[1]
    core = lax.axis_index("c")
    block = lax.axis_index("ctx")
    head = (2 * lax.axis_index("x") + core) * heads // (H // KVH)
    columns = pl.ds(pl.multiple_of(head * HD, HD), HD)
    tokens_copy = pltpu.make_async_copy(tokens_hbm, tokens, sems.at[0])
    tokens_copy.start()

    @pl.when(core == 0)
    def _():
        pltpu.make_async_copy(w_key.at[:, columns], weight, sems.at[1]).start()

    @pl.when(core != 0)
    def _():
        pltpu.make_async_copy(w_value.at[:, columns], weight, sems.at[1]).start()

    counts = lengths[...].astype(jnp.float32)
    before = iota((docs, docs), 1) <= iota((docs, docs), 0)
    ends = jnp.sum(jnp.where(before, counts, 0.0), axis=1, keepdims=True)
    here = (block * rows + iota((docs, rows), 1)).astype(jnp.float32)
    start_row = jnp.max(jnp.where(ends <= here, ends, 0.0), axis=0, keepdims=True)
    same = iota((rows, rows), 0) == iota((rows, rows), 1)
    start_column = jnp.sum(jnp.where(same, start_row, 0.0), axis=1, keepdims=True)
    starts[...] = start_column.astype(jnp.int32)
    span[0] = jnp.min(start_row).astype(jnp.int32)
    span[1] = jnp.max(start_row).astype(jnp.int32)
    offsets = (block * rows + iota((rows, 1), 0)).astype(jnp.float32) - start_column
    half = rows // 2
    lower = iota((half, HD), 1) < HD // 2
    angles = jnp.where(lower, offsets[:half], offsets[half:]) * frequency[...]
    for table, wave in ((cosine, jnp.cos(angles)), (sine, jnp.sin(angles))):
        other = pltpu.roll(wave, HD // 2, 1)
        sign = -1.0 if table is sine else 1.0
        table[:half] = jnp.where(lower, sign * wave, other)
        table[half:] = jnp.where(lower, sign * other, wave)

    tokens_copy.wait()
    pltpu.make_async_copy(w_key.at[:, columns], weight, sems.at[1]).wait()
    u = jnp.dot(tokens[...], weight[...], preferred_element_type=jnp.float32)

    @pl.when(core == 0)
    def _():
        out[...] = norm_rotate(u, gain[...], cosine[...], sine[...]).astype(out.dtype)

    @pl.when(core != 0)
    def _():
        out[...] = u.astype(out.dtype)


def project_kv(tokens, w_key, w_value, gain, lengths, heads):
    rows, width = tokens.shape
    frequency = jnp.asarray(np.tile(FREQUENCY, 2)[None], jnp.float32)
    table = jax.ShapeDtypeStruct((rows, HD), jnp.float32)
    return pl.pallas_call(
        functools.partial(kv_body, heads),
        out_shape=(
            jax.ShapeDtypeStruct((rows, HD), jnp.bfloat16),
            table,
            table,
            jax.ShapeDtypeStruct((rows, 1), jnp.int32),
            jax.ShapeDtypeStruct((2,), jnp.int32),
        ),
        in_specs=[pl.BlockSpec(memory_space=pltpu.HBM)] * 3
        + [pl.BlockSpec(memory_space=VMEM)] * 3,
        out_specs=(pl.BlockSpec(memory_space=VMEM),) * 4
        + (pl.BlockSpec(memory_space=pltpu.SMEM),),
        scratch_shapes=[
            VMEM((rows, width), tokens.dtype),
            VMEM((width, HD), w_key.dtype),
            pltpu.SemaphoreType.DMA((2,)),
        ],
        cost_estimate=pl.CostEstimate(
            flops=2 * rows * width * HD, bytes_accessed=4 * rows * width, transcendentals=0
        ),
        compiler_params=pltpu.CompilerParams(vmem_limit_bytes=63 << 20),
        name="project_kv",
    )(tokens, w_key, w_value, gain, lengths, frequency)


def q_body(tokens_hbm, w_hbm, gain, cosine_any, sine_any, out, tokens, weight, cosine, sine, sems):
    wide = weight.shape[2]
    copies = [
        pltpu.make_async_copy(tokens_hbm, tokens, sems.at[0]),
        pltpu.make_async_copy(w_hbm.at[:, pl.ds(0, wide)], weight.at[0], sems.at[1]),
        pltpu.make_async_copy(cosine_any, cosine, sems.at[2]),
        pltpu.make_async_copy(sine_any, sine, sems.at[3]),
    ]
    later = []
    for i in range(1, weight.shape[0]):
        later.append(
            pltpu.make_async_copy(
                w_hbm.at[:, pl.ds(i * wide, wide)], weight.at[i], sems.at[3 + i]
            )
        )
    for copy in copies + later:
        copy.start()
    for copy in copies:
        copy.wait()
    each = wide // HD
    for i in range(weight.shape[0]):
        if i > 0:
            later[i - 1].wait()
        u = jnp.dot(tokens[...], weight[i], preferred_element_type=jnp.float32)
        for h in range(each):
            part = u[:, h * HD : (h + 1) * HD]
            turned = norm_rotate(part, gain[...], cosine[...], sine[...])
            out[i * each + h] = turned.astype(out.dtype)


def project_q(tokens, w_query, gain, cosine, sine):
    rows, width = tokens.shape
    heads = w_query.shape[1] // HD
    chunks = 2
    return pl.pallas_call(
        q_body,
        out_shape=jax.ShapeDtypeStruct((heads, rows, HD), jnp.bfloat16),
        in_specs=[pl.BlockSpec(memory_space=pltpu.HBM)] * 2
        + [pl.BlockSpec(memory_space=VMEM)]
        + [pl.BlockSpec(memory_space=pl.ANY)] * 2,
        out_specs=pl.BlockSpec(memory_space=VMEM),
        scratch_shapes=[
            VMEM((rows, width), tokens.dtype),
            VMEM((chunks, width, heads * HD // chunks), w_query.dtype),
            VMEM((rows, HD), jnp.float32),
            VMEM((rows, HD), jnp.float32),
            pltpu.SemaphoreType.DMA((3 + chunks,)),
        ],
        cost_estimate=pl.CostEstimate(
            flops=2 * rows * width * heads * HD, bytes_accessed=6 * rows * width, transcendentals=0
        ),
        compiler_params=pltpu.CompilerParams(vmem_limit_bytes=63 << 20),
        name="project_q",
    )(tokens, w_query, gain, cosine, sine)


def scored(query, key):
    return lax.dot_general(
        query, key, (((1,), (1,)), ((), ())), preferred_element_type=jnp.float32
    )


def add_block(heads, queries, key, value, total, weighted, mask):
    scores = scored(queries[0], key)
    for h in range(heads):
        following = scored(queries[h + 1], key) if h + 1 < heads else None
        weights = jnp.exp2(scores * (HD**-0.5 * LOG2E))
        if mask is not None:
            weights = weights * mask[...]
        sums = weights[:, :HD]
        for at in range(HD, weights.shape[1], HD):
            sums = sums + weights[:, at : at + HD]
        total[h] += sums
        weighted[h] += jnp.dot(
            weights.astype(jnp.bfloat16), value, preferred_element_type=jnp.float32
        )
        scores = following


def add_blocks(heads, distance_of, deepest, span, queries, starts, kv, total, weighted, mask):
    rows = queries.shape[1]
    places = kv.shape[1]
    block = lax.axis_index("ctx")
    first = span[0] // rows
    last = span[1]

    def step(place, carry):
        b = block - distance_of(place)

        @pl.when(b >= first)
        def _():
            key, value = kv[0, place], kv[1, place]
            whole = (b < block) & (b * rows >= last)

            @pl.when(whole)
            def _():
                add_block(heads, queries, key, value, total, weighted, None)

            @pl.when(jnp.logical_not(whole))
            def _():
                key_pos = b * rows + iota((rows, rows), 1)
                query_pos = block * rows + iota((rows, rows), 0)
                visible = (key_pos <= query_pos) & (key_pos >= starts[...])
                mask[...] = jnp.where(visible, 1.0, 0.0)
                add_block(heads, queries, key, value, total, weighted, mask)

        return carry

    together = (places == LINE) & ((block - deepest) * rows >= last) & (deepest > 0)

    if places == LINE:

        @pl.when(together)
        def _():
            four = pl.ds(places - LINE, LINE)
            key = kv[0, four].reshape(LINE * rows, HD)
            value = kv[1, four].reshape(LINE * rows, HD)
            add_block(heads, queries, key, value, total, weighted, None)

    lax.fori_loop(0, jnp.where(together, places - LINE, places), step, 0)


def start_copies(mine, theirs, kv, sems):
    core = lax.axis_index("c")
    copies = []
    for side, group in ((core, mine), (1 - core, theirs)):
        at = 0
        for ref in group:
            count = ref.shape[0]
            copies.append(
                pltpu.make_async_copy(
                    ref, kv.at[side, pl.ds(at, count)], sems.at[len(copies)]
                )
            )
            at += count
    for copy in copies:
        copy.start()
    return copies


def near_body(heads, first_call, distance_of, deepest, n, span, queries, starts, *refs):
    if not first_call:
        total_in, weighted_in, refs = refs[0], refs[1], refs[2:]
    mine, theirs = refs[:n], refs[n : 2 * n]
    total, weighted, mask, kv, sems = refs[2 * n :]
    copies = start_copies(mine, theirs, kv, sems)
    if first_call:
        total[...] = jnp.zeros_like(total)
        weighted[...] = jnp.zeros_like(weighted)
    else:
        total[...] = total_in[...]
        weighted[...] = weighted_in[...]
    for copy in copies:
        copy.wait()
    add_blocks(
        heads, distance_of, deepest, span, queries, starts, kv, total, weighted, mask
    )


def attend_near(span, queries, starts, state, mine, theirs, distance_of, deepest):
    heads, rows, _ = queries.shape
    n = len(mine)
    places = sum(a.shape[0] for a in mine)
    shape = jax.ShapeDtypeStruct((heads, rows, HD), jnp.float32)
    return pl.pallas_call(
        functools.partial(near_body, heads, not state, distance_of, deepest, n),
        out_shape=(shape, shape),
        in_specs=[pl.BlockSpec(memory_space=pltpu.SMEM)]
        + [pl.BlockSpec(memory_space=VMEM)] * (2 + len(state))
        + [pl.BlockSpec(memory_space=pl.ANY)] * (2 * n),
        out_specs=(pl.BlockSpec(memory_space=VMEM),) * 2,
        scratch_shapes=[
            VMEM((rows, rows), jnp.float32),
            VMEM((2, places, rows, HD), jnp.bfloat16),
            pltpu.SemaphoreType.DMA((2 * n,)),
        ],
        cost_estimate=pl.CostEstimate(
            flops=4 * places * heads * rows * rows * HD, bytes_accessed=2 << 20, transcendentals=0
        ),
        compiler_params=pltpu.CompilerParams(vmem_limit_bytes=12 << 20),
    )(span, queries, starts, *state, *mine, *theirs)


def far_body(heads, n, span, queries, starts, total_in, weighted_in, *refs):
    mine, theirs = refs[:n], refs[n : 2 * n]
    w_out_any, keep, give, total, weighted, mask, attended, kv, w_out, sems = refs[2 * n :]
    copies = start_copies(mine, theirs, kv, sems)
    weights_copy = pltpu.make_async_copy(w_out_any, w_out, sems.at[2 * n])
    weights_copy.start()
    core = lax.axis_index("c")
    total[...] = total_in[...]
    weighted[...] = weighted_in[...]
    for copy in copies:
        copy.wait()

    deepest = 0

    def distance_of(place):
        return REACH + place

    add_blocks(
        heads, distance_of, deepest, span, queries, starts, kv, total, weighted, mask
    )
    for h in range(heads):
        sums = jnp.sum(total[h], axis=1, keepdims=True)
        attended[:, h * HD : (h + 1) * HD] = (weighted[h] / sums).astype(attended.dtype)
    weights_copy.wait()
    width = keep.shape[2]
    for out, side in ((give, 1 - core), (keep, core)):
        for x in range(keep.shape[0]):
            columns = pl.ds(pl.multiple_of((2 * x + side) * width, width), width)
            out[x] = jnp.dot(
                attended[...], w_out[:, columns], preferred_element_type=jnp.float32
            ).astype(out.dtype)


def attend_far(span, queries, starts, total, weighted, mine, theirs, w_out, chips):
    heads, rows, _ = queries.shape
    n = len(mine)
    places = sum(a.shape[0] for a in mine)
    width = w_out.shape[1] // (2 * chips)
    half = jax.ShapeDtypeStruct((chips, rows, width), jnp.bfloat16)
    return pl.pallas_call(
        functools.partial(far_body, heads, n),
        out_shape=(half, half),
        in_specs=[pl.BlockSpec(memory_space=pltpu.SMEM)]
        + [pl.BlockSpec(memory_space=VMEM)] * 4
        + [pl.BlockSpec(memory_space=pl.ANY)] * (2 * n + 1),
        out_specs=(pl.BlockSpec(memory_space=VMEM),) * 2,
        scratch_shapes=[
            VMEM((heads, rows, HD), jnp.float32),
            VMEM((heads, rows, HD), jnp.float32),
            VMEM((rows, rows), jnp.float32),
            VMEM((rows, heads * HD), jnp.bfloat16),
            VMEM((2, places, rows, HD), jnp.bfloat16),
            VMEM(w_out.shape, jnp.bfloat16),
            pltpu.SemaphoreType.DMA((2 * n + 1,)),
        ],
        cost_estimate=pl.CostEstimate(
            flops=4 * places * heads * rows * rows * HD, bytes_accessed=4 << 20, transcendentals=0
        ),
        compiler_params=pltpu.CompilerParams(vmem_limit_bytes=16 << 20),
        name="attend_far",
    )(span, queries, starts, total, weighted, *mine, *theirs, w_out)


def passed_along(a, distance):
    n = lax.axis_size("ctx")
    return lax.ppermute(a, "ctx", [(i, i + distance) for i in range(n - distance)])


def swapped(a):
    return lax.ppermute(a, "c", [(0, 1), (1, 0)])


def local(tokens, w_query, w_key, w_value, w_out, query_gain, key_gain, doc_lengths):
    heads = w_query.shape[1] // HD
    chips = lax.axis_size("x")
    part, cosine, sine, starts, span = project_kv(
        tokens, w_key, w_value, key_gain[None], doc_lengths[None], heads
    )
    own = part[None]
    far = [passed_along(part, LINE + 1)]
    near = passed_along(part, 1)
    theirs = [swapped(own)]
    for _ in range(2):
        far.append(passed_along(far[-1], LINE))
    queries = project_q(tokens, w_query, query_gain[None], cosine, sine)
    early = jnp.stack([near] + far[:2])
    moved = passed_along(early, 1)
    theirs.append(swapped(early))
    hops = [jnp.concatenate([moved, far[2][None]])]
    for i in range(LINE - 1):
        moving = hops[-1] if i < LINE - 2 else hops[-1][LINE - 1 :]
        hops.append(passed_along(moving, 1))
        theirs = theirs + [swapped(hops[-2])]
    mine = [own, early] + hops
    theirs.append(swapped(hops[-1]))
    state = ()
    for i, (low, high) in enumerate(((0, 2), (2, 3), (3, 4), (4, 5))):

        def distance_of(place, i=i):
            if i == 0:
                return jnp.where(place == 0, 0, 1 + LINE * (place - 1))
            return jnp.where(place == LINE - 1, 12 + i, 1 + i + LINE * place)

        state = attend_near(
            span, queries, starts, state, mine[low:high], theirs[low:high],
            distance_of, 12 + i if i else 0,
        )
    total, weighted = state
    keep, give = attend_far(
        span, queries, starts, total, weighted, mine[5:], theirs[5:], w_out, chips
    )
    pairs = (keep.astype(jnp.float32) + swapped(give).astype(jnp.float32)).astype(jnp.bfloat16)
    terms = lax.all_to_all(pairs, "x", 0, 0, tiled=True)
    return jnp.sum(terms.astype(jnp.float32), axis=0).astype(jnp.bfloat16)


def solution(mesh):
    ctx, tp = mesh.shape["ctx"], mesh.shape["tp"]
    fine = Mesh(mesh.devices.reshape(ctx, tp // 2, 2), ("ctx",) + TP)
    return jax.shard_map(
        local,
        mesh=fine,
        in_specs=(P("ctx", None), P(None, TP), P(), P(), P(TP, None), P(), P(), P()),
        out_specs=P("ctx", TP),
        check_vma=False,
    )
```
